128 devices in a mesh: rack: 4 (over x_hi, core), node: 32 (over y, x_lo, z).
Axes of the slice: x: 4 (x_hi: 2, x_lo: 2; x = x_hi * 2 + x_lo), y: 4, z: 4, core: 2. Of those that a mesh axis runs over, the one named last changes fastest.
Arguments:
- stored: bfloat16 [2560, 8, 4096], P(('rack', 'node')), may hold values from -6 to 6
- coefficients: bfloat16 [256, 10, 8, 8], replicated, may hold values from -0.3 to 0.61
- helper_rack: int32 [256, 10], replicated, may hold values from 0 to 3, as said below
- helper_node: int32 [256, 10], replicated, may hold values from 0 to 31, as said below
- helper_block: int32 [256, 10], replicated, may hold values from 0 to 19, as said below
Outputs:
- rebuilt: float32 [256, 8, 4096], P(('rack', 'node'))
The draws below stay inside these ranges and needn't reach their ends.
Inputs may be any that keep to these rules, and one draw needn't show every extreme that they name: Repair r is rebuilt on device r // 2, counted rack-major. Its 10 helpers are distinct devices other than that one. With devices counted rack-major as helper_rack * 32 + helper_node, (helper device minus owner device) mod (128) depends only on h and r mod 2. `helper_node`: follows the same rule as helper_rack. `helper_block`: each of a device's 20 stored blocks is read by exactly one pair of repair and helper.
All inputs are finite; a program needn't handle non-finite values.
Results may differ from the reference program's by a relative error of at most 0.0003.
Values sent between devices are 32-bit elements; how exact they have to be, the bound alone decides.
No kernel may reach another device: no remote copies, remote signals or barrier semaphores. Data moves between devices by JAX's collectives and lax.ppermute only.
A program may use at most 64 MiB of HBM per device.

```python
import math
import jax
import jax.numpy as jnp
from jax import lax

PLANES = 8
HELPERS = 10
REP_DEV = 2
REPAIRS = 256
HOLD = 20
LEN = 4096
N_RACK = 4
N_NODE = 32


def permute_slots(perm_key):
    return jax.random.permutation(perm_key, HOLD)


def routing(key):
    devices = N_RACK * N_NODE
    offset_keys = jax.random.split(jax.random.fold_in(key, 7001), REP_DEV)
    offsets = jnp.stack([jax.random.permutation(offset_keys[slot], devices - 1)[:HELPERS] + 1 for slot in range(REP_DEV)]).astype(jnp.int32)
    repair_ids = jnp.arange(REPAIRS, dtype=jnp.int32)
    owner = repair_ids // REP_DEV
    position = repair_ids % REP_DEV
    device = (owner[:, None] + offsets[position]) % devices
    rack = device // N_NODE
    node = device % N_NODE
    perm_keys = jax.random.split(jax.random.fold_in(key, 7002), devices)
    slot_perms = jax.vmap(permute_slots)(perm_keys).astype(jnp.int32)
    columns = jnp.arange(HELPERS, dtype=jnp.int32)[None, :] * REP_DEV + position[:, None]
    block = slot_perms[device, columns]
    return (rack.astype(jnp.int32), node.astype(jnp.int32), block.astype(jnp.int32))


def draw_helper_rack(key, part):
    return routing(key)[0]


def draw_helper_node(key, part):
    return routing(key)[1]


def draw_helper_block(key, part):
    return routing(key)[2]


def draw_coefficients(key, part):
    noise_key = jax.random.fold_in(key, 7003)
    shape = (REPAIRS, HELPERS, PLANES, PLANES)
    noise = jnp.clip(jax.random.normal(noise_key, shape, jnp.float32), -3.0, 3.0) * 0.3
    identity = jnp.eye(PLANES, dtype=jnp.float32)
    return ((identity + noise) / math.sqrt(HELPERS)).astype(jnp.bfloat16)


def block_levels(rng, shape, pieces, low, largest):
    factor_of, own = 1.0, jax.random.fold_in(rng, 6)
    for axis_at, shards_of in pieces:
        draws = jnp.exp(jax.random.uniform(jax.random.fold_in(own, axis_at), (shards_of,), jnp.float32, low / len(pieces), largest / len(pieces)))
        factor_of = factor_of * jnp.repeat(draws, shape[axis_at] // shards_of).reshape([-1 if axis == axis_at else 1 for axis in range(len(shape))])
    return factor_of


def scatter_about(rng, extent, width, most, pieces=(), kind=jnp.bfloat16):
    result = width * jax.random.normal(rng, extent, jnp.float32)
    if pieces:
        result = result * block_levels(rng, extent, pieces, -0.22, 0.18)
    return jnp.clip(result, -most, most).astype(kind)


def setup_inputs(seed: int = 0) -> dict:
    key_of = jax.random.split(jax.random.key(seed), 6)
    return {
        "stored": scatter_about(key_of[0], (N_RACK * N_NODE * HOLD, PLANES, LEN), 1.0, 6.0, ((0, 128),)),
        "coefficients": draw_coefficients(jax.random.fold_in(key_of[5], 71), 0),
        "helper_rack": draw_helper_rack(jax.random.fold_in(key_of[5], 71), 0),
        "helper_node": draw_helper_node(jax.random.fold_in(key_of[5], 71), 0),
        "helper_block": draw_helper_block(jax.random.fold_in(key_of[5], 71), 0),
    }


def reference(stored, coefficients, helper_rack, helper_node, helper_block):
    source_rows = ((helper_rack * N_NODE + helper_node) * HOLD + helper_block).astype(jnp.int32)

    def repair(packed):
        row_index, coeffs = packed
        partial_value = jnp.zeros((PLANES, LEN), jnp.float32)
        for helper_pos in range(HELPERS):
            source = stored[row_index[helper_pos]].astype(jnp.float32)
            partial_value = partial_value + jnp.dot(coeffs[helper_pos].astype(jnp.float32), source, precision=lax.Precision.HIGHEST)
        return partial_value

    return lax.map(repair, (source_rows, coefficients))
```

```python
import jax
import jax.numpy as jnp
from jax import lax
from jax.sharding import PartitionSpec as P

HELPERS = 10
REP_DEV = 2
AXES = ("rack", "node")


def on_device(stored, coefficients, helper_rack, helper_node, helper_block):
    node_count = lax.axis_size("node")
    device_count = lax.axis_size(AXES)
    planes, length = stored.shape[1:]
    my_device = lax.axis_index("rack") * node_count + lax.axis_index("node")
    offsets = (helper_rack[:REP_DEV] * node_count + helper_node[:REP_DEV]) % device_count
    owner = (my_device - offsets) % device_count
    position = jnp.arange(REP_DEV, dtype=jnp.int32)[:, None]
    repair_rows = owner * REP_DEV + position
    helper_slot = jnp.arange(HELPERS, dtype=jnp.int32)[None, :]
    local_rows = helper_block[repair_rows, helper_slot]
    coeffs_used = coefficients[repair_rows, helper_slot]
    blocks_used = stored[local_rows]
    contrib = jnp.einsum(
        "shpq,shql->shpl", coeffs_used, blocks_used, preferred_element_type=jnp.float32
    )
    terms = REP_DEV * HELPERS
    share = planes * length // device_count
    lanes = 128
    sent = contrib.reshape(terms, device_count, share).transpose(1, 0, 2)
    sent = sent.reshape(device_count, terms * share // lanes, lanes)
    held = lax.all_to_all(sent, AXES, 0, 0, tiled=True)
    held = held.reshape(device_count, terms, share // lanes, lanes)
    twice = jnp.concatenate([held, held], 0)
    sums = []
    for s in range(REP_DEV):
        total = None
        for h in range(HELPERS):
            part = lax.dynamic_slice(
                twice, (offsets[s, h], s * HELPERS + h, 0, 0), (device_count, 1, share // lanes, lanes)
            )
            total = part if total is None else total + part
        sums.append(total)
    back = jnp.concatenate(sums, 1).reshape(device_count, REP_DEV * share // lanes, lanes)
    rebuilt = lax.all_to_all(back, AXES, 0, 0, tiled=True)
    rebuilt = rebuilt.reshape(device_count, REP_DEV, share).transpose(1, 0, 2)
    return rebuilt.reshape(REP_DEV, planes, length)


def solution(mesh):
    placed = (P(AXES, None, None), P(), P(), P(), P())
    return jax.shard_map(
        on_device,
        mesh=mesh,
        in_specs=placed,
        out_specs=P(AXES, None, None),
        check_vma=False,
    )
```

```python
import jax
import jax.numpy as jnp
from jax import lax
from jax.experimental import pallas as pl
from jax.experimental.pallas import tpu as pltpu
from jax.sharding import PartitionSpec as P

HELPERS = 10
REP_DEV = 2
AXES = ("rack", "node")
LANES = 128
TILE = 8


def offset_of(rack_ref, node_ref, node_count, device_count, s, h):
    return lax.rem(rack_ref[h, s] * node_count + node_ref[h, s], device_count)


def make_terms(node_count, device_count, me_ref, rack_ref, node_ref, slots_ref, coeff_ref, stored_ref,
               out_ref, weight):
    held, planes, columns = stored_ref.shape
    terms = REP_DEV * HELPERS

    @pl.when(pl.program_id(0) == 0)
    def _():
        me = me_ref[0]
        repairs = slots_ref.shape[1]
        width = weight.shape[0] * LANES
        entries = planes * planes
        table = coeff_ref[...].astype(jnp.float32).reshape(HELPERS * entries, repairs).astype(jnp.bfloat16)
        repair = lax.broadcasted_iota(jnp.int32, (HELPERS, repairs), 1)
        own = lax.div(lax.broadcasted_iota(jnp.int32, (HELPERS, HELPERS * entries), 1), entries) == (
            lax.broadcasted_iota(jnp.int32, (HELPERS, HELPERS * entries), 0)
        )
        fold = (
            lax.rem(lax.broadcasted_iota(jnp.int32, (HELPERS * entries, entries), 0), entries)
            == lax.broadcasted_iota(jnp.int32, (HELPERS * entries, entries), 1)
        ).astype(jnp.bfloat16)
        entry = lax.broadcasted_iota(jnp.int32, (entries, width), 0)
        lane = lax.broadcasted_iota(jnp.int32, (entries, width), 1)
        slot_of_lane = lax.div(lax.broadcasted_iota(jnp.int32, (HELPERS, width), 1), planes)
        picked, slots = [], []
        for s in range(REP_DEV):
            offset = lax.rem(rack_ref[:, s : s + 1] * node_count + node_ref[:, s : s + 1], device_count)
            row = lax.rem(me + device_count - offset, device_count) * REP_DEV + s
            chosen = row == repair
            slots.append(jnp.sum(jnp.where(chosen, slots_ref[...], 0), axis=1, keepdims=True))
            every = lax.dot_general(
                chosen.astype(jnp.float32).astype(jnp.bfloat16), table, (((1,), (1,)), ((), ())),
                preferred_element_type=jnp.float32,
            )
            every = jnp.where(own, every, 0.0).astype(jnp.bfloat16)
            picked.append(jnp.dot(every, fold, preferred_element_type=jnp.float32).astype(jnp.bfloat16))
        for p in range(planes):
            spread = (entry == p * planes + lax.rem(lane, planes)).astype(jnp.float32).astype(jnp.bfloat16)
            for s in range(REP_DEV):
                wide = jnp.dot(picked[s], spread, preferred_element_type=jnp.float32)
                wide = jnp.where(slots[s] == slot_of_lane, wide, 0.0)
                first = p * terms + s * HELPERS
                for w in range(weight.shape[0]):
                    weight[w, first : first + HELPERS, :] = wide[:, w * LANES : (w + 1) * LANES]

    blocks = stored_ref[...].astype(jnp.float32).reshape(held * planes, columns).astype(jnp.bfloat16)
    matrix = jnp.concatenate([weight[w] for w in range(weight.shape[0])], 1)[:, : held * planes].astype(jnp.bfloat16)
    result = jnp.dot(matrix, blocks, preferred_element_type=jnp.float32)
    for j in range(columns // LANES):
        out_ref[j] = result[:, j * LANES : (j + 1) * LANES]


def add_terms(node_count, device_count, rack_ref, node_ref, held_hbm, out_ref, held, sems):
    terms = REP_DEV * HELPERS
    per = held_hbm.shape[0] // device_count
    parts = per // terms
    main = pltpu.make_async_copy(held_hbm, held.at[pl.ds(0, device_count * per)], sems.at[0])
    wrap = pltpu.make_async_copy(
        held_hbm.at[pl.ds(0, TILE * per)], held.at[pl.ds(device_count * per, TILE * per)], sems.at[1]
    )
    main.start()
    wrap.start()
    offsets = [offset_of(rack_ref, node_ref, node_count, device_count, k // HELPERS, k % HELPERS) for k in range(terms)]
    main.wait()
    wrap.wait()

    @pl.loop(0, device_count // TILE)
    def _(j):
        starts = [lax.rem(j * TILE + offset, device_count) * per for offset in offsets]
        for s in range(REP_DEV):
            for i in range(parts):
                total = None
                for h in range(HELPERS):
                    k = s * HELPERS + h
                    part = held[pl.ds(starts[k] + (i * terms + k), TILE, stride=per), :]
                    total = part if total is None else total + part
                out_ref[pl.ds(j * TILE * parts * REP_DEV + i * REP_DEV + s, TILE, stride=parts * REP_DEV), :] = total


def place(in_ref, out_ref):
    planes, length = out_ref.shape[1:]
    for s in range(REP_DEV):
        for t in range(length // LANES):
            tile = in_ref[pl.ds(t * planes * REP_DEV + s, planes, stride=REP_DEV), :]
            out_ref[s, :, t * LANES : (t + 1) * LANES] = tile


def on_device(stored, coefficients, helper_rack, helper_node, helper_block):
    node_count = lax.axis_size("node")
    device_count = lax.axis_size(AXES)
    held, planes, length = stored.shape
    terms = REP_DEV * HELPERS
    me = (lax.axis_index("rack") * node_count + lax.axis_index("node")).reshape(1)
    tiles = length // LANES
    step = 4
    racks, nodes, slots = helper_rack.T, helper_node.T, helper_block.T
    table = coefficients.transpose(1, 2, 3, 0)
    index_spec = pl.BlockSpec((HELPERS, LANES), lambda *_: (0, 0), memory_space=pltpu.SMEM)
    sent = pl.pallas_call(
        lambda *refs: make_terms(node_count, device_count, *refs),
        out_shape=jax.ShapeDtypeStruct((tiles, planes * terms, LANES), jnp.float32),
        grid=(tiles // step,),
        in_specs=[
            pl.BlockSpec(memory_space=pltpu.SMEM),
            pl.BlockSpec((HELPERS, LANES), lambda g: (0, 0)),
            pl.BlockSpec((HELPERS, LANES), lambda g: (0, 0)),
            pl.BlockSpec(slots.shape, lambda g: (0, 0)),
            pl.BlockSpec(table.shape, lambda g: (0, 0, 0, 0)),
            pl.BlockSpec((held, planes, step * LANES), lambda g: (0, 0, g)),
        ],
        out_specs=pl.BlockSpec((step, planes * terms, LANES), lambda g: (g, 0, 0)),
        scratch_shapes=[pltpu.VMEM((pl.cdiv(held * planes, LANES), planes * terms, LANES), jnp.float32)],
        name="make_terms",
    )(me, racks, nodes, slots, table, stored)
    per = tiles * planes * terms // device_count
    arrived = lax.all_to_all(sent.reshape(device_count, per, LANES), AXES, 0, 0, tiled=True)
    parts = per // terms
    back = pl.pallas_call(
        lambda *refs: add_terms(node_count, device_count, *refs),
        out_shape=jax.ShapeDtypeStruct((device_count * parts * REP_DEV, LANES), jnp.float32),
        grid=(1,),
        in_specs=[index_spec, index_spec, pl.BlockSpec(memory_space=pl.ANY)],
        out_specs=pl.BlockSpec((device_count * parts * REP_DEV, LANES), lambda g: (0, 0)),
        scratch_shapes=[
            pltpu.VMEM(((device_count + TILE) * per, LANES), jnp.float32),
            pltpu.SemaphoreType.DMA((2,)),
        ],
        name="add_terms",
    )(racks, nodes, arrived.reshape(device_count * per, LANES))
    home = lax.all_to_all(back.reshape(device_count, parts * REP_DEV, LANES), AXES, 0, 0, tiled=True)
    return pl.pallas_call(
        place,
        out_shape=jax.ShapeDtypeStruct((REP_DEV, planes, length), jnp.float32),
        name="place",
    )(home.reshape(device_count * parts * REP_DEV, LANES))


def solution(mesh):
    placed = (P(AXES, None, None), P(), P(), P(), P())
    return jax.shard_map(
        on_device,
        mesh=mesh,
        in_specs=placed,
        out_specs=P(AXES, None, None),
        check_vma=False,
    )
```

```python
import jax
import jax.numpy as jnp
from jax import lax
from jax.experimental import pallas as pl
from jax.experimental.pallas import tpu as pltpu
from jax.sharding import PartitionSpec as P

HELPERS = 10
REP_DEV = 2
AXES = ("rack", "node")
LANES = 128
TILE = 8


def offset_of(rack_ref, node_ref, node_count, device_count, s, h):
    return lax.rem(rack_ref[h, s] * node_count + node_ref[h, s], device_count)


def make_terms(node_count, device_count, me_ref, rack_ref, node_ref, slots_ref, coeff_ref, stored_ref,
               out_ref, weight):
    held, planes, columns = stored_ref.shape
    terms = REP_DEV * HELPERS

    @pl.when(pl.program_id(0) == 0)
    def _():
        me = me_ref[0]
        repairs = slots_ref.shape[1]
        width = weight.shape[0] * LANES
        entries = planes * planes
        table = coeff_ref[...].astype(jnp.float32).reshape(HELPERS * entries, repairs).astype(jnp.bfloat16)
        repair = lax.broadcasted_iota(jnp.int32, (HELPERS, repairs), 1)
        own = lax.div(lax.broadcasted_iota(jnp.int32, (HELPERS, HELPERS * entries), 1), entries) == (
            lax.broadcasted_iota(jnp.int32, (HELPERS, HELPERS * entries), 0)
        )
        fold = (
            lax.rem(lax.broadcasted_iota(jnp.int32, (HELPERS * entries, entries), 0), entries)
            == lax.broadcasted_iota(jnp.int32, (HELPERS * entries, entries), 1)
        ).astype(jnp.bfloat16)
        entry = lax.broadcasted_iota(jnp.int32, (entries, width), 0)
        lane = lax.broadcasted_iota(jnp.int32, (entries, width), 1)
        slot_of_lane = lax.div(lax.broadcasted_iota(jnp.int32, (HELPERS, width), 1), planes)
        picked, slots = [], []
        for s in range(REP_DEV):
            offset = lax.rem(rack_ref[:, s : s + 1] * node_count + node_ref[:, s : s + 1], device_count)
            row = lax.rem(me + device_count - offset, device_count) * REP_DEV + s
            chosen = row == repair
            slots.append(jnp.sum(jnp.where(chosen, slots_ref[...], 0), axis=1, keepdims=True))
            every = lax.dot_general(
                chosen.astype(jnp.float32).astype(jnp.bfloat16), table, (((1,), (1,)), ((), ())),
                preferred_element_type=jnp.float32,
            )
            every = jnp.where(own, every, 0.0).astype(jnp.bfloat16)
            picked.append(jnp.dot(every, fold, preferred_element_type=jnp.float32).astype(jnp.bfloat16))
        for p in range(planes):
            spread = (entry == p * planes + lax.rem(lane, planes)).astype(jnp.float32).astype(jnp.bfloat16)
            for s in range(REP_DEV):
                wide = jnp.dot(picked[s], spread, preferred_element_type=jnp.float32)
                wide = jnp.where(slots[s] == slot_of_lane, wide, 0.0)
                first = p * terms + s * HELPERS
                for w in range(weight.shape[0]):
                    weight[w, first : first + HELPERS, :] = wide[:, w * LANES : (w + 1) * LANES]

    blocks = stored_ref[...].astype(jnp.float32).reshape(held * planes, columns).astype(jnp.bfloat16)
    matrix = jnp.concatenate([weight[w] for w in range(weight.shape[0])], 1)[:, : held * planes].astype(jnp.bfloat16)
    result = jnp.dot(matrix, blocks, preferred_element_type=jnp.float32)
    for j in range(columns // LANES):
        out_ref[j] = result[:, j * LANES : (j + 1) * LANES]


def add_terms(node_count, device_count, rack_ref, node_ref, held_hbm, out_ref, held, sems):
    terms = REP_DEV * HELPERS
    per = held_hbm.shape[0] // device_count
    parts = per // terms
    main = pltpu.make_async_copy(held_hbm, held.at[pl.ds(0, device_count * per)], sems.at[0])
    wrap = pltpu.make_async_copy(
        held_hbm.at[pl.ds(0, TILE * per)], held.at[pl.ds(device_count * per, TILE * per)], sems.at[1]
    )
    main.start()
    wrap.start()
    offsets = [offset_of(rack_ref, node_ref, node_count, device_count, k // HELPERS, k % HELPERS) for k in range(terms)]
    main.wait()
    wrap.wait()

    @pl.loop(0, device_count // TILE)
    def _(j):
        starts = [lax.rem(j * TILE + offset, device_count) * per for offset in offsets]
        for s in range(REP_DEV):
            for i in range(parts):
                total = None
                for h in range(HELPERS):
                    k = s * HELPERS + h
                    part = held[pl.ds(starts[k] + (i * terms + k), TILE, stride=per), :]
                    total = part if total is None else total + part
                out_ref[pl.ds(j * TILE * parts * REP_DEV + i * REP_DEV + s, TILE, stride=parts * REP_DEV), :] = total


def place(in_ref, out_ref):
    planes, length = out_ref.shape[1:]
    for s in range(REP_DEV):
        for t in range(length // LANES):
            tile = in_ref[pl.ds(t * planes * REP_DEV + s, planes, stride=REP_DEV), :]
            out_ref[s, :, t * LANES : (t + 1) * LANES] = tile


def on_device(stored, coefficients, helper_rack, helper_node, helper_block):
    node_count = lax.axis_size("node")
    device_count = lax.axis_size(AXES)
    held, planes, length = stored.shape
    terms = REP_DEV * HELPERS
    me = (lax.axis_index("rack") * node_count + lax.axis_index("node")).reshape(1)
    tiles = length // LANES
    step = 4
    racks, nodes, slots = helper_rack.T, helper_node.T, helper_block.T
    table = coefficients.transpose(1, 2, 3, 0)
    stored, table, racks, nodes, slots = (
        pltpu.with_memory_space_constraint(x, pltpu.HBM) for x in (stored, table, racks, nodes, slots)
    )
    index_spec = pl.BlockSpec((HELPERS, LANES), lambda *_: (0, 0), memory_space=pltpu.SMEM)
    sent = pl.pallas_call(
        lambda *refs: make_terms(node_count, device_count, *refs),
        out_shape=jax.ShapeDtypeStruct((tiles, planes * terms, LANES), jnp.float32),
        grid=(tiles // step,),
        in_specs=[
            pl.BlockSpec(memory_space=pltpu.SMEM),
            pl.BlockSpec((HELPERS, LANES), lambda g: (0, 0)),
            pl.BlockSpec((HELPERS, LANES), lambda g: (0, 0)),
            pl.BlockSpec(slots.shape, lambda g: (0, 0)),
            pl.BlockSpec(table.shape, lambda g: (0, 0, 0, 0)),
            pl.BlockSpec((held, planes, step * LANES), lambda g: (0, 0, g)),
        ],
        out_specs=pl.BlockSpec((step, planes * terms, LANES), lambda g: (g, 0, 0)),
        scratch_shapes=[pltpu.VMEM((pl.cdiv(held * planes, LANES), planes * terms, LANES), jnp.float32)],
        compiler_params=pltpu.CompilerParams(vmem_limit_bytes=12 << 20),
        name="make_terms",
    )(me, racks, nodes, slots, table, stored)
    per = tiles * planes * terms // device_count
    arrived = lax.all_to_all(sent.reshape(device_count, per, LANES), AXES, 0, 0, tiled=True)
    parts = per // terms
    back = pl.pallas_call(
        lambda *refs: add_terms(node_count, device_count, *refs),
        out_shape=jax.ShapeDtypeStruct((device_count * parts * REP_DEV, LANES), jnp.float32),
        grid=(1,),
        in_specs=[index_spec, index_spec, pl.BlockSpec(memory_space=pl.ANY)],
        out_specs=pl.BlockSpec((device_count * parts * REP_DEV, LANES), lambda g: (0, 0)),
        scratch_shapes=[
            pltpu.VMEM(((device_count + TILE) * per, LANES), jnp.float32),
            pltpu.SemaphoreType.DMA((2,)),
        ],
        compiler_params=pltpu.CompilerParams(vmem_limit_bytes=12 << 20),
        name="add_terms",
    )(racks, nodes, arrived.reshape(device_count * per, LANES))
    home = lax.all_to_all(back.reshape(device_count, parts * REP_DEV, LANES), AXES, 0, 0, tiled=True)
    return pl.pallas_call(
        place,
        out_shape=jax.ShapeDtypeStruct((REP_DEV, planes, length), jnp.float32),
        compiler_params=pltpu.CompilerParams(vmem_limit_bytes=4 << 20),
        name="place",
    )(home.reshape(device_count * parts * REP_DEV, LANES))


def solution(mesh):
    placed = (P(AXES, None, None), P(), P(), P(), P())
    return jax.shard_map(
        on_device,
        mesh=mesh,
        in_specs=placed,
        out_specs=P(AXES, None, None),
        check_vma=False,
    )
```

```python
import jax
import jax.numpy as jnp
from jax import lax
from jax.experimental import pallas as pl
from jax.experimental.pallas import tpu as pltpu
from jax.sharding import PartitionSpec as P

HELPERS = 10
REP_DEV = 2
AXES = ("rack", "node")
LANES = 128
TILE = 8


def offset_of(rack_ref, node_ref, node_count, device_count, s, h):
    return lax.rem(rack_ref[h, s] * node_count + node_ref[h, s], device_count)


def make_terms(node_count, device_count, me_ref, rack_ref, node_ref, slots_ref, coeff_ref, stored_ref,
               out_ref, weight):
    held, planes, columns = stored_ref.shape
    terms = REP_DEV * HELPERS

    @pl.when(pl.program_id(0) == 0)
    def _():
        me = me_ref[0]
        repairs = slots_ref.shape[1]
        width = weight.shape[0] * LANES
        entries = planes * planes
        table = coeff_ref[...].astype(jnp.float32).reshape(HELPERS * entries, repairs).astype(jnp.bfloat16)
        repair = lax.broadcasted_iota(jnp.int32, (HELPERS, repairs), 1)
        own = lax.div(lax.broadcasted_iota(jnp.int32, (HELPERS, HELPERS * entries), 1), entries) == (
            lax.broadcasted_iota(jnp.int32, (HELPERS, HELPERS * entries), 0)
        )
        fold = (
            lax.rem(lax.broadcasted_iota(jnp.int32, (HELPERS * entries, entries), 0), entries)
            == lax.broadcasted_iota(jnp.int32, (HELPERS * entries, entries), 1)
        ).astype(jnp.bfloat16)
        entry = lax.broadcasted_iota(jnp.int32, (entries, width), 0)
        lane = lax.broadcasted_iota(jnp.int32, (entries, width), 1)
        slot_of_lane = lax.div(lax.broadcasted_iota(jnp.int32, (HELPERS, width), 1), planes)
        picked, slots = [], []
        for s in range(REP_DEV):
            offset = lax.rem(rack_ref[:, s : s + 1] * node_count + node_ref[:, s : s + 1], device_count)
            row = lax.rem(me + device_count - offset, device_count) * REP_DEV + s
            chosen = row == repair
            slots.append(jnp.sum(jnp.where(chosen, slots_ref[...], 0), axis=1, keepdims=True))
            every = lax.dot_general(
                chosen.astype(jnp.float32).astype(jnp.bfloat16), table, (((1,), (1,)), ((), ())),
                preferred_element_type=jnp.float32,
            )
            every = jnp.where(own, every, 0.0).astype(jnp.bfloat16)
            picked.append(jnp.dot(every, fold, preferred_element_type=jnp.float32).astype(jnp.bfloat16))
        for p in range(planes):
            spread = (entry == p * planes + lax.rem(lane, planes)).astype(jnp.float32).astype(jnp.bfloat16)
            for s in range(REP_DEV):
                wide = jnp.dot(picked[s], spread, preferred_element_type=jnp.float32)
                wide = jnp.where(slots[s] == slot_of_lane, wide, 0.0)
                first = p * terms + s * HELPERS
                for w in range(weight.shape[0]):
                    weight[w, first : first + HELPERS, :] = wide[:, w * LANES : (w + 1) * LANES]

    blocks = stored_ref[...].astype(jnp.float32).reshape(held * planes, columns).astype(jnp.bfloat16)
    matrix = jnp.concatenate([weight[w] for w in range(weight.shape[0])], 1)[:, : held * planes].astype(jnp.bfloat16)
    result = jnp.dot(matrix, blocks, preferred_element_type=jnp.float32)
    for j in range(columns // LANES):
        out_ref[j] = result[:, j * LANES : (j + 1) * LANES]


def add_terms(node_count, device_count, rack_ref, node_ref, held_hbm, out_ref, held, sems):
    terms = REP_DEV * HELPERS
    per = held_hbm.shape[0] // device_count
    parts = per // terms
    main = pltpu.make_async_copy(held_hbm, held.at[pl.ds(0, device_count * per)], sems.at[0])
    wrap = pltpu.make_async_copy(
        held_hbm.at[pl.ds(0, TILE * per)], held.at[pl.ds(device_count * per, TILE * per)], sems.at[1]
    )
    main.start()
    wrap.start()
    offsets = [offset_of(rack_ref, node_ref, node_count, device_count, k // HELPERS, k % HELPERS) for k in range(terms)]
    main.wait()
    wrap.wait()

    @pl.loop(0, device_count // TILE)
    def _(j):
        starts = [lax.rem(j * TILE + offset, device_count) * per for offset in offsets]
        for s in range(REP_DEV):
            for i in range(parts):
                total = None
                for h in range(HELPERS):
                    k = s * HELPERS + h
                    part = held[pl.ds(starts[k] + (i * terms + k), TILE, stride=per), :]
                    total = part if total is None else total + part
                out_ref[pl.ds(j * TILE * parts * REP_DEV + i * REP_DEV + s, TILE, stride=parts * REP_DEV), :] = total


def place(in_ref, out_ref):
    planes, length = out_ref.shape[1:]
    for s in range(REP_DEV):
        for t in range(length // LANES):
            tile = in_ref[pl.ds(t * planes * REP_DEV + s, planes, stride=REP_DEV), :]
            out_ref[s, :, t * LANES : (t + 1) * LANES] = tile


def on_device(stored, coefficients, helper_rack, helper_node, helper_block):
    node_count = lax.axis_size("node")
    device_count = lax.axis_size(AXES)
    held, planes, length = stored.shape
    terms = REP_DEV * HELPERS
    me = (lax.axis_index("rack") * node_count + lax.axis_index("node")).reshape(1)
    tiles = length // LANES
    step = 16
    racks, nodes, slots = helper_rack.T, helper_node.T, helper_block.T
    table = coefficients.transpose(1, 2, 3, 0)
    stored, table, racks, nodes, slots = (
        pltpu.with_memory_space_constraint(x, pltpu.HBM) for x in (stored, table, racks, nodes, slots)
    )
    index_spec = pl.BlockSpec((HELPERS, LANES), lambda *_: (0, 0), memory_space=pltpu.SMEM)
    sent = pl.pallas_call(
        lambda *refs: make_terms(node_count, device_count, *refs),
        out_shape=jax.ShapeDtypeStruct((tiles, planes * terms, LANES), jnp.float32),
        grid=(tiles // step,),
        in_specs=[
            pl.BlockSpec(memory_space=pltpu.SMEM),
            pl.BlockSpec((HELPERS, LANES), lambda g: (0, 0)),
            pl.BlockSpec((HELPERS, LANES), lambda g: (0, 0)),
            pl.BlockSpec(slots.shape, lambda g: (0, 0)),
            pl.BlockSpec(table.shape, lambda g: (0, 0, 0, 0)),
            pl.BlockSpec((held, planes, step * LANES), lambda g: (0, 0, g)),
        ],
        out_specs=pl.BlockSpec((step, planes * terms, LANES), lambda g: (g, 0, 0)),
        scratch_shapes=[pltpu.VMEM((pl.cdiv(held * planes, LANES), planes * terms, LANES), jnp.float32)],
        compiler_params=pltpu.CompilerParams(vmem_limit_bytes=12 << 20),
        name="make_terms",
    )(me, racks, nodes, slots, table, stored)
    per = tiles * planes * terms // device_count
    arrived = lax.all_to_all(sent.reshape(device_count, per, LANES), AXES, 0, 0, tiled=True)
    parts = per // terms
    back = pl.pallas_call(
        lambda *refs: add_terms(node_count, device_count, *refs),
        out_shape=jax.ShapeDtypeStruct((device_count * parts * REP_DEV, LANES), jnp.float32),
        grid=(1,),
        in_specs=[index_spec, index_spec, pl.BlockSpec(memory_space=pl.ANY)],
        out_specs=pl.BlockSpec((device_count * parts * REP_DEV, LANES), lambda g: (0, 0)),
        scratch_shapes=[
            pltpu.VMEM(((device_count + TILE) * per, LANES), jnp.float32),
            pltpu.SemaphoreType.DMA((2,)),
        ],
        compiler_params=pltpu.CompilerParams(vmem_limit_bytes=12 << 20),
        name="add_terms",
    )(racks, nodes, arrived.reshape(device_count * per, LANES))
    home = lax.all_to_all(back.reshape(device_count, parts * REP_DEV, LANES), AXES, 0, 0, tiled=True)
    return pl.pallas_call(
        place,
        out_shape=jax.ShapeDtypeStruct((REP_DEV, planes, length), jnp.float32),
        compiler_params=pltpu.CompilerParams(vmem_limit_bytes=4 << 20),
        name="place",
    )(home.reshape(device_count * parts * REP_DEV, LANES))


def solution(mesh):
    placed = (P(AXES, None, None), P(), P(), P(), P())
    return jax.shard_map(
        on_device,
        mesh=mesh,
        in_specs=placed,
        out_specs=P(AXES, None, None),
        check_vma=False,
    )
```

```python
import jax
import jax.numpy as jnp
from jax import lax
from jax.experimental import pallas as pl
from jax.experimental.pallas import tpu as pltpu
from jax.sharding import PartitionSpec as P

HELPERS = 10
REP_DEV = 2
AXES = ("rack", "node")
LANES = 128
TILE = 8


def offset_of(rack_ref, node_ref, node_count, device_count, s, h):
    return lax.rem(rack_ref[h, s] * node_count + node_ref[h, s], device_count)


def make_terms(node_count, device_count, me_ref, rack_hbm, node_hbm, slots_hbm, coeff_hbm, stored_hbm,
               out_ref, racks, nodes, all_slots, coeffs, blocks, weight, sems):
    chunks, held_planes, columns = blocks.shape
    tiles = columns // LANES
    terms = REP_DEV * HELPERS
    planes = held_planes // terms
    index = [
        pltpu.make_async_copy(source, target, sems.at[n])
        for n, (source, target) in enumerate(
            ((rack_hbm.at[:, pl.ds(0, LANES)], racks), (node_hbm.at[:, pl.ds(0, LANES)], nodes),
             (slots_hbm, all_slots), (coeff_hbm, coeffs))
        )
    ]
    for copy in index:
        copy.start()
    loads = [
        pltpu.make_async_copy(stored_hbm.at[:, pl.ds(c * columns, columns)], blocks.at[c], sems.at[len(index) + c])
        for c in range(chunks)
    ]
    for copy in loads:
        copy.start()
    me = me_ref[0]
    repairs = all_slots.shape[1]
    width = weight.shape[0] * LANES
    entries = planes * planes
    repair = lax.broadcasted_iota(jnp.int32, (HELPERS, repairs), 1)
    own = lax.div(lax.broadcasted_iota(jnp.int32, (HELPERS, HELPERS * entries), 1), entries) == (
        lax.broadcasted_iota(jnp.int32, (HELPERS, HELPERS * entries), 0)
    )
    fold = (
        lax.rem(lax.broadcasted_iota(jnp.int32, (HELPERS * entries, entries), 0), entries)
        == lax.broadcasted_iota(jnp.int32, (HELPERS * entries, entries), 1)
    ).astype(jnp.bfloat16)
    entry = lax.broadcasted_iota(jnp.int32, (entries, width), 0)
    lane = lax.broadcasted_iota(jnp.int32, (entries, width), 1)
    slot_of_lane = lax.div(lax.broadcasted_iota(jnp.int32, (HELPERS, width), 1), planes)
    for copy in index:
        copy.wait()
    table = coeffs[...].astype(jnp.float32).reshape(HELPERS * entries, repairs).astype(jnp.bfloat16)
    picked, slots = [], []
    for s in range(REP_DEV):
        offset = lax.rem(racks[:, s : s + 1] * node_count + nodes[:, s : s + 1], device_count)
        row = lax.rem(me + device_count - offset, device_count) * REP_DEV + s
        chosen = row == repair
        slots.append(jnp.sum(jnp.where(chosen, all_slots[...], 0), axis=1, keepdims=True))
        every = lax.dot_general(
            chosen.astype(jnp.float32).astype(jnp.bfloat16), table, (((1,), (1,)), ((), ())),
            preferred_element_type=jnp.float32,
        )
        every = jnp.where(own, every, 0.0).astype(jnp.bfloat16)
        picked.append(jnp.dot(every, fold, preferred_element_type=jnp.float32).astype(jnp.bfloat16))
    for p in range(planes):
        spread = (entry == p * planes + lax.rem(lane, planes)).astype(jnp.float32).astype(jnp.bfloat16)
        for s in range(REP_DEV):
            wide = jnp.dot(picked[s], spread, preferred_element_type=jnp.float32)
            wide = jnp.where(slots[s] == slot_of_lane, wide, 0.0)
            first = (s * planes + p) * HELPERS
            for w in range(weight.shape[0]):
                weight[w, first : first + HELPERS, :] = wide[:, w * LANES : (w + 1) * LANES]
    matrix = jnp.concatenate([weight[w] for w in range(weight.shape[0])], 1)[:, :held_planes].astype(jnp.bfloat16)
    for c in range(chunks):
        loads[c].wait()
        result = jnp.dot(matrix, blocks[c], preferred_element_type=jnp.float32)
        for j in range(tiles):
            for s in range(REP_DEV):
                out_ref[s, c * tiles + j] = result[s * planes * HELPERS : (s + 1) * planes * HELPERS, j * LANES : (j + 1) * LANES]


def add_terms(node_count, device_count, me_ref, rack_ref, node_ref, held_hbm, out_ref, held, sems):
    per = held_hbm.shape[0] // device_count
    parts = per // HELPERS
    main = pltpu.make_async_copy(held_hbm, held.at[pl.ds(0, device_count * per)], sems.at[0])
    wrap = pltpu.make_async_copy(
        held_hbm.at[pl.ds(0, TILE * per)], held.at[pl.ds(device_count * per, TILE * per)], sems.at[1]
    )
    main.start()
    wrap.start()
    s = lax.div(me_ref[0], device_count // REP_DEV)
    offsets = [lax.rem(rack_ref[h, s] * node_count + node_ref[h, s], device_count) for h in range(HELPERS)]
    main.wait()
    wrap.wait()

    @pl.loop(0, device_count // TILE)
    def _(j):
        starts = [lax.rem(j * TILE + offset, device_count) * per for offset in offsets]
        for i in range(parts):
            total = None
            for h in range(HELPERS):
                part = held[pl.ds(starts[h] + (i * HELPERS + h), TILE, stride=per), :]
                total = part if total is None else total + part
            out_ref[pl.ds(j * TILE * parts + i, TILE, stride=parts), :] = total


def on_device(stored, coefficients, helper_rack, helper_node, helper_block):
    node_count = lax.axis_size("node")
    device_count = lax.axis_size(AXES)
    held, planes, length = stored.shape
    terms = REP_DEV * HELPERS
    me = (lax.axis_index("rack") * node_count + lax.axis_index("node")).reshape(1)
    tiles = length // LANES
    chunks = 2
    racks, nodes, slots = helper_rack.T, helper_node.T, helper_block.T
    table = coefficients.transpose(1, 2, 3, 0)
    blocks = stored.reshape(held * planes, length)
    index_spec = pl.BlockSpec((HELPERS, LANES), lambda *_: (0, 0), memory_space=pltpu.SMEM)
    sent = pl.pallas_call(
        lambda *refs: make_terms(node_count, device_count, *refs),
        out_shape=jax.ShapeDtypeStruct((REP_DEV, tiles, planes * HELPERS, LANES), jnp.float32),
        in_specs=[pl.BlockSpec(memory_space=pltpu.SMEM)] + [pl.BlockSpec(memory_space=pl.ANY)] * 5,
        out_specs=pl.BlockSpec(memory_space=pltpu.VMEM),
        scratch_shapes=[
            pltpu.VMEM((HELPERS, LANES), jnp.int32),
            pltpu.VMEM((HELPERS, LANES), jnp.int32),
            pltpu.VMEM(slots.shape, jnp.int32),
            pltpu.VMEM(table.shape, table.dtype),
            pltpu.VMEM((chunks, held * planes, length // chunks), stored.dtype),
            pltpu.VMEM((pl.cdiv(held * planes, LANES), planes * terms, LANES), jnp.float32),
            pltpu.SemaphoreType.DMA((4 + chunks,)),
        ],
        compiler_params=pltpu.CompilerParams(vmem_limit_bytes=12 << 20),
        name="make_terms",
    )(me, *(pltpu.with_memory_space_constraint(x, pltpu.HBM) for x in (racks, nodes, slots, table, blocks)))
    per = REP_DEV * tiles * planes * HELPERS // device_count
    arrived = lax.all_to_all(sent.reshape(device_count, per, LANES), AXES, 0, 0, tiled=True)
    parts = per // HELPERS
    back = pl.pallas_call(
        lambda *refs: add_terms(node_count, device_count, *refs),
        out_shape=jax.ShapeDtypeStruct((device_count * parts, LANES), jnp.float32),
        grid=(1,),
        in_specs=[pl.BlockSpec(memory_space=pltpu.SMEM), index_spec, index_spec, pl.BlockSpec(memory_space=pl.ANY)],
        out_specs=pl.BlockSpec((device_count * parts, LANES), lambda g: (0, 0)),
        scratch_shapes=[
            pltpu.VMEM(((device_count + TILE) * per, LANES), jnp.float32),
            pltpu.SemaphoreType.DMA((2,)),
        ],
        compiler_params=pltpu.CompilerParams(vmem_limit_bytes=12 << 20),
        name="add_terms",
    )(me, racks, nodes, arrived.reshape(device_count * per, LANES))
    home = lax.all_to_all(back.reshape(device_count, parts, LANES), AXES, 0, 0, tiled=True)
    home = home.reshape(REP_DEV, tiles, planes, LANES).transpose(0, 2, 1, 3)
    return home.reshape(REP_DEV, planes, length)


def solution(mesh):
    placed = (P(AXES, None, None), P(), P(), P(), P())
    return jax.shard_map(
        on_device,
        mesh=mesh,
        in_specs=placed,
        out_specs=P(AXES, None, None),
        check_vma=False,
    )
```

```python
import jax
import jax.numpy as jnp
from jax import lax
from jax.experimental import pallas as pl
from jax.experimental.pallas import tpu as pltpu
from jax.sharding import PartitionSpec as P

HELPERS = 10
REP_DEV = 2
AXES = ("rack", "node")
LANES = 128
TILE = 8


def offset_of(rack_ref, node_ref, node_count, device_count, s, h):
    return lax.rem(rack_ref[h, s] * node_count + node_ref[h, s], device_count)


def make_terms(node_count, device_count, me_ref, rack_hbm, node_hbm, slots_hbm, coeff_hbm, stored_hbm,
               out_ref, racks, nodes, all_slots, coeffs, blocks, weight, sems):
    chunks, held_planes, columns = blocks.shape
    tiles = columns // LANES
    terms = REP_DEV * HELPERS
    planes = held_planes // terms
    index = [
        pltpu.make_async_copy(source, target, sems.at[n])
        for n, (source, target) in enumerate(
            ((rack_hbm.at[:, pl.ds(0, LANES)], racks), (node_hbm.at[:, pl.ds(0, LANES)], nodes),
             (slots_hbm, all_slots), (coeff_hbm, coeffs))
        )
    ]
    for copy in index:
        copy.start()
    loads = [
        pltpu.make_async_copy(stored_hbm.at[:, pl.ds(c * columns, columns)], blocks.at[c], sems.at[len(index) + c])
        for c in range(chunks)
    ]
    for copy in loads:
        copy.start()
    me = me_ref[0]
    repairs = all_slots.shape[1]
    width = weight.shape[0] * LANES
    entries = planes * planes
    repair = lax.broadcasted_iota(jnp.int32, (HELPERS, repairs), 1)
    own = lax.div(lax.broadcasted_iota(jnp.int32, (HELPERS, HELPERS * entries), 1), entries) == (
        lax.broadcasted_iota(jnp.int32, (HELPERS, HELPERS * entries), 0)
    )
    fold = (
        lax.rem(lax.broadcasted_iota(jnp.int32, (HELPERS * entries, entries), 0), entries)
        == lax.broadcasted_iota(jnp.int32, (HELPERS * entries, entries), 1)
    ).astype(jnp.bfloat16)
    entry = lax.broadcasted_iota(jnp.int32, (entries, width), 0)
    lane = lax.broadcasted_iota(jnp.int32, (entries, width), 1)
    slot_of_lane = lax.div(lax.broadcasted_iota(jnp.int32, (HELPERS, width), 1), planes)
    for copy in index:
        copy.wait()
    table = coeffs[...].astype(jnp.float32).reshape(HELPERS * entries, repairs).astype(jnp.bfloat16)
    picked, slots = [], []
    for s in range(REP_DEV):
        offset = lax.rem(racks[:, s : s + 1] * node_count + nodes[:, s : s + 1], device_count)
        row = lax.rem(me + device_count - offset, device_count) * REP_DEV + s
        chosen = row == repair
        slots.append(jnp.sum(jnp.where(chosen, all_slots[...], 0), axis=1, keepdims=True))
        every = lax.dot_general(
            chosen.astype(jnp.float32).astype(jnp.bfloat16), table, (((1,), (1,)), ((), ())),
            preferred_element_type=jnp.float32,
        )
        every = jnp.where(own, every, 0.0).astype(jnp.bfloat16)
        picked.append(jnp.dot(every, fold, preferred_element_type=jnp.float32).astype(jnp.bfloat16))
    for p in range(planes):
        spread = (entry == p * planes + lax.rem(lane, planes)).astype(jnp.float32).astype(jnp.bfloat16)
        for s in range(REP_DEV):
            wide = jnp.dot(picked[s], spread, preferred_element_type=jnp.float32)
            wide = jnp.where(slots[s] == slot_of_lane, wide, 0.0)
            first = (s * planes + p) * HELPERS
            for w in range(weight.shape[0]):
                weight[w, first : first + HELPERS, :] = wide[:, w * LANES : (w + 1) * LANES]
    matrix = jnp.concatenate([weight[w] for w in range(weight.shape[0])], 1)[:, :held_planes].astype(jnp.bfloat16)
    for c in range(chunks):
        loads[c].wait()
        result = jnp.dot(matrix, blocks[c], preferred_element_type=jnp.float32)
        for j in range(tiles):
            for s in range(REP_DEV):
                out_ref[s, c * tiles + j] = result[s * planes * HELPERS : (s + 1) * planes * HELPERS, j * LANES : (j + 1) * LANES]


def add_terms(node_count, device_count, me_ref, rack_any, node_any, held_any, out_ref, racks, nodes, held, sems):
    per = held_any.shape[0] // device_count
    parts = per // HELPERS
    index = [
        pltpu.make_async_copy(source.at[:, pl.ds(0, LANES)], target, sems.at[n])
        for n, (source, target) in enumerate(((rack_any, racks), (node_any, nodes)))
    ]
    main = pltpu.make_async_copy(held_any, held.at[pl.ds(0, device_count * per)], sems.at[2])
    wrap = pltpu.make_async_copy(
        held_any.at[pl.ds(0, TILE * per)], held.at[pl.ds(device_count * per, TILE * per)], sems.at[3]
    )
    for copy in index:
        copy.start()
    main.start()
    wrap.start()
    for copy in index:
        copy.wait()
    s = lax.div(me_ref[0], device_count // REP_DEV)
    offsets = [lax.rem(racks[h, s] * node_count + nodes[h, s], device_count) for h in range(HELPERS)]
    main.wait()
    wrap.wait()

    @pl.loop(0, device_count // TILE)
    def _(j):
        starts = [lax.rem(j * TILE + offset, device_count) * per for offset in offsets]
        for i in range(parts):
            total = None
            for h in range(HELPERS):
                part = held[pl.ds(starts[h] + (i * HELPERS + h), TILE, stride=per), :]
                total = part if total is None else total + part
            out_ref[pl.ds(j * TILE * parts + i, TILE, stride=parts), :] = total


def on_device(stored, coefficients, helper_rack, helper_node, helper_block):
    node_count = lax.axis_size("node")
    device_count = lax.axis_size(AXES)
    held, planes, length = stored.shape
    terms = REP_DEV * HELPERS
    me = (lax.axis_index("rack") * node_count + lax.axis_index("node")).reshape(1)
    tiles = length // LANES
    chunks = 1
    racks, nodes, slots = helper_rack.T, helper_node.T, helper_block.T
    table = coefficients.transpose(1, 2, 3, 0)
    blocks = stored.reshape(held * planes, length)
    sent = pl.pallas_call(
        lambda *refs: make_terms(node_count, device_count, *refs),
        out_shape=jax.ShapeDtypeStruct((REP_DEV, tiles, planes * HELPERS, LANES), jnp.float32),
        in_specs=[pl.BlockSpec(memory_space=pltpu.SMEM)] + [pl.BlockSpec(memory_space=pl.ANY)] * 5,
        out_specs=pl.BlockSpec(memory_space=pltpu.VMEM),
        scratch_shapes=[
            pltpu.VMEM((HELPERS, LANES), jnp.int32),
            pltpu.VMEM((HELPERS, LANES), jnp.int32),
            pltpu.VMEM(slots.shape, jnp.int32),
            pltpu.VMEM(table.shape, table.dtype),
            pltpu.VMEM((chunks, held * planes, length // chunks), stored.dtype),
            pltpu.VMEM((pl.cdiv(held * planes, LANES), planes * terms, LANES), jnp.float32),
            pltpu.SemaphoreType.DMA((4 + chunks,)),
        ],
        compiler_params=pltpu.CompilerParams(vmem_limit_bytes=12 << 20),
        name="make_terms",
    )(me, *(pltpu.with_memory_space_constraint(x, pltpu.HBM) for x in (racks, nodes, slots, table, blocks)))
    per = REP_DEV * tiles * planes * HELPERS // device_count
    arrived = lax.all_to_all(sent.reshape(device_count, per, LANES), AXES, 0, 0, tiled=True)
    parts = per // HELPERS
    back = pl.pallas_call(
        lambda *refs: add_terms(node_count, device_count, *refs),
        out_shape=jax.ShapeDtypeStruct((device_count * parts, LANES), jnp.float32),
        in_specs=[pl.BlockSpec(memory_space=pltpu.SMEM)] + [pl.BlockSpec(memory_space=pl.ANY)] * 3,
        out_specs=pl.BlockSpec(memory_space=pltpu.VMEM),
        scratch_shapes=[
            pltpu.SMEM((HELPERS, LANES), jnp.int32),
            pltpu.SMEM((HELPERS, LANES), jnp.int32),
            pltpu.VMEM(((device_count + TILE) * per, LANES), jnp.float32),
            pltpu.SemaphoreType.DMA((4,)),
        ],
        compiler_params=pltpu.CompilerParams(vmem_limit_bytes=12 << 20),
        name="add_terms",
    )(me, racks, nodes, arrived.reshape(device_count * per, LANES))
    home = lax.all_to_all(back.reshape(device_count, parts, LANES), AXES, 0, 0, tiled=True)
    home = home.reshape(REP_DEV, tiles, planes, LANES).transpose(0, 2, 1, 3)
    return home.reshape(REP_DEV, planes, length)


def solution(mesh):
    placed = (P(AXES, None, None), P(), P(), P(), P())
    return jax.shard_map(
        on_device,
        mesh=mesh,
        in_specs=placed,
        out_specs=P(AXES, None, None),
        check_vma=False,
    )
```

```python
import jax
import jax.numpy as jnp
from jax import lax
from jax.experimental import pallas as pl
from jax.experimental.pallas import tpu as pltpu
from jax.sharding import PartitionSpec as P

HELPERS = 10
REP_DEV = 2
AXES = ("rack", "node")
LANES = 128
TILE = 8
TURN = 101


def offset_of(rack_ref, node_ref, node_count, device_count, s, h):
    return lax.rem(rack_ref[h, s] * node_count + node_ref[h, s], device_count)


def make_terms(node_count, device_count, me_ref, rack_hbm, node_hbm, slots_hbm, coeff_hbm, stored_hbm,
               out_ref, racks, nodes, all_slots, coeffs, blocks, weight, sems):
    chunks, held_planes, columns = blocks.shape
    tiles = columns // LANES
    terms = REP_DEV * HELPERS
    planes = held_planes // terms
    index = [
        pltpu.make_async_copy(source, target, sems.at[n])
        for n, (source, target) in enumerate(
            ((rack_hbm.at[:, pl.ds(0, LANES)], racks), (node_hbm.at[:, pl.ds(0, LANES)], nodes),
             (slots_hbm, all_slots), (coeff_hbm, coeffs))
        )
    ]
    for copy in index:
        copy.start()
    loads = [
        pltpu.make_async_copy(stored_hbm.at[:, pl.ds(c * columns, columns)], blocks.at[c], sems.at[len(index) + c])
        for c in range(chunks)
    ]
    for copy in loads:
        copy.start()
    me = me_ref[0]
    repairs = all_slots.shape[1]
    width = weight.shape[0] * LANES
    entries = planes * planes
    repair = lax.broadcasted_iota(jnp.int32, (HELPERS, repairs), 1)
    own = lax.div(lax.broadcasted_iota(jnp.int32, (HELPERS, HELPERS * entries), 1), entries) == (
        lax.broadcasted_iota(jnp.int32, (HELPERS, HELPERS * entries), 0)
    )
    fold = (
        lax.rem(lax.broadcasted_iota(jnp.int32, (HELPERS * entries, entries), 0), entries)
        == lax.broadcasted_iota(jnp.int32, (HELPERS * entries, entries), 1)
    ).astype(jnp.bfloat16)
    entry = lax.broadcasted_iota(jnp.int32, (entries, width), 0)
    lane = lax.broadcasted_iota(jnp.int32, (entries, width), 1)
    slot_of_lane = lax.div(lax.broadcasted_iota(jnp.int32, (HELPERS, width), 1), planes)
    for copy in index:
        copy.wait()
    table = coeffs[...].astype(jnp.float32).reshape(HELPERS * entries, repairs).astype(jnp.bfloat16)
    picked, slots = [], []
    for s in range(REP_DEV):
        offset = lax.rem(racks[:, s : s + 1] * node_count + nodes[:, s : s + 1], device_count)
        row = lax.rem(me + device_count - offset, device_count) * REP_DEV + s
        chosen = row == repair
        slots.append(jnp.sum(jnp.where(chosen, all_slots[...], 0), axis=1, keepdims=True))
        every = lax.dot_general(
            chosen.astype(jnp.float32).astype(jnp.bfloat16), table, (((1,), (1,)), ((), ())),
            preferred_element_type=jnp.float32,
        )
        every = jnp.where(own, every, 0.0).astype(jnp.bfloat16)
        picked.append(jnp.dot(every, fold, preferred_element_type=jnp.float32).astype(jnp.bfloat16))
    for p in range(planes):
        spread = (entry == p * planes + lax.rem(lane, planes)).astype(jnp.float32).astype(jnp.bfloat16)
        for s in range(REP_DEV):
            wide = jnp.dot(picked[s], spread, preferred_element_type=jnp.float32)
            wide = jnp.where(slots[s] == slot_of_lane, wide, 0.0)
            first = (s * planes + p) * HELPERS
            for w in range(weight.shape[0]):
                weight[w, first : first + HELPERS, :] = wide[:, w * LANES : (w + 1) * LANES]
    matrix = jnp.concatenate([weight[w] for w in range(weight.shape[0])], 1)[:, :held_planes].astype(jnp.bfloat16)
    for c in range(chunks):
        loads[c].wait()
        result = jnp.dot(matrix, blocks[c], preferred_element_type=jnp.float32)
        for j in range(tiles):
            for s in range(REP_DEV):
                out_ref[s, c * tiles + j] = result[s * planes * HELPERS : (s + 1) * planes * HELPERS, j * LANES : (j + 1) * LANES]


def add_terms(node_count, device_count, me_ref, rack_any, node_any, held_any, out_ref, racks, nodes, held, sems):
    per = held_any.shape[0] // device_count
    parts = per // HELPERS
    index = [
        pltpu.make_async_copy(source.at[:, pl.ds(0, LANES)], target, sems.at[n])
        for n, (source, target) in enumerate(((rack_any, racks), (node_any, nodes)))
    ]
    main = pltpu.make_async_copy(held_any, held.at[pl.ds(0, device_count * per)], sems.at[2])
    wrap = pltpu.make_async_copy(
        held_any.at[pl.ds(0, TILE * per)], held.at[pl.ds(device_count * per, TILE * per)], sems.at[3]
    )
    for copy in index:
        copy.start()
    main.start()
    wrap.start()
    for copy in index:
        copy.wait()
    turn = TURN % device_count
    s = lax.div(lax.rem(me_ref[0] * turn, device_count), device_count // REP_DEV)
    offsets = [lax.rem((racks[h, s] * node_count + nodes[h, s]) * turn, device_count) for h in range(HELPERS)]
    main.wait()
    wrap.wait()

    @pl.loop(0, device_count // TILE)
    def _(j):
        starts = [lax.rem(j * TILE + offset, device_count) * per for offset in offsets]
        for i in range(parts):
            total = None
            for h in range(HELPERS):
                part = held[pl.ds(starts[h] + (i * HELPERS + h), TILE, stride=per), :]
                total = part if total is None else total + part
            out_ref[pl.ds(j * TILE * parts + i, TILE, stride=parts), :] = total


def ring(count):
    order = [0] * count
    for device in range(count):
        order[device * TURN % count] = device
    return [order]


def on_device(stored, coefficients, helper_rack, helper_node, helper_block):
    node_count = lax.axis_size("node")
    device_count = lax.axis_size(AXES)
    held, planes, length = stored.shape
    terms = REP_DEV * HELPERS
    me = (lax.axis_index("rack") * node_count + lax.axis_index("node")).reshape(1)
    tiles = length // LANES
    chunks = 1
    racks, nodes, slots = helper_rack.T, helper_node.T, helper_block.T
    table = coefficients.transpose(1, 2, 3, 0)
    blocks = stored.reshape(held * planes, length)
    sent = pl.pallas_call(
        lambda *refs: make_terms(node_count, device_count, *refs),
        out_shape=jax.ShapeDtypeStruct((REP_DEV, tiles, planes * HELPERS, LANES), jnp.float32),
        in_specs=[pl.BlockSpec(memory_space=pltpu.SMEM)] + [pl.BlockSpec(memory_space=pl.ANY)] * 5,
        out_specs=pl.BlockSpec(memory_space=pltpu.VMEM),
        scratch_shapes=[
            pltpu.VMEM((HELPERS, LANES), jnp.int32),
            pltpu.VMEM((HELPERS, LANES), jnp.int32),
            pltpu.VMEM(slots.shape, jnp.int32),
            pltpu.VMEM(table.shape, table.dtype),
            pltpu.VMEM((chunks, held * planes, length // chunks), stored.dtype),
            pltpu.VMEM((pl.cdiv(held * planes, LANES), planes * terms, LANES), jnp.float32),
            pltpu.SemaphoreType.DMA((4 + chunks,)),
        ],
        compiler_params=pltpu.CompilerParams(vmem_limit_bytes=12 << 20),
        name="make_terms",
    )(me, *(pltpu.with_memory_space_constraint(x, pltpu.HBM) for x in (racks, nodes, slots, table, blocks)))
    per = REP_DEV * tiles * planes * HELPERS // device_count
    arrived = lax.all_to_all(sent.reshape(device_count, per, LANES), AXES, 0, 0, tiled=True, axis_index_groups=ring(device_count))
    parts = per // HELPERS
    back = pl.pallas_call(
        lambda *refs: add_terms(node_count, device_count, *refs),
        out_shape=jax.ShapeDtypeStruct((device_count * parts, LANES), jnp.float32),
        in_specs=[pl.BlockSpec(memory_space=pltpu.SMEM)] + [pl.BlockSpec(memory_space=pl.ANY)] * 3,
        out_specs=pl.BlockSpec(memory_space=pltpu.VMEM),
        scratch_shapes=[
            pltpu.SMEM((HELPERS, LANES), jnp.int32),
            pltpu.SMEM((HELPERS, LANES), jnp.int32),
            pltpu.VMEM(((device_count + TILE) * per, LANES), jnp.float32),
            pltpu.SemaphoreType.DMA((4,)),
        ],
        compiler_params=pltpu.CompilerParams(vmem_limit_bytes=12 << 20),
        name="add_terms",
    )(me, racks, nodes, arrived.reshape(device_count * per, LANES))
    home = lax.all_to_all(back.reshape(device_count, parts, LANES), AXES, 0, 0, tiled=True, axis_index_groups=ring(device_count))
    home = home.reshape(REP_DEV, tiles, planes, LANES).transpose(0, 2, 1, 3)
    return home.reshape(REP_DEV, planes, length)


def solution(mesh):
    placed = (P(AXES, None, None), P(), P(), P(), P())
    return jax.shard_map(
        on_device,
        mesh=mesh,
        in_specs=placed,
        out_specs=P(AXES, None, None),
        check_vma=False,
    )
```

```python
import jax
import jax.numpy as jnp
from jax import lax
from jax.experimental import pallas as pl
from jax.experimental.pallas import tpu as pltpu
from jax.sharding import PartitionSpec as P

HELPERS = 10
REP_DEV = 2
AXES = ("rack", "node")
LANES = 128
TILE = 8
TURN = 101
PIECES = 1


def offset_of(rack_ref, node_ref, node_count, device_count, s, h):
    return lax.rem(rack_ref[h, s] * node_count + node_ref[h, s], device_count)


def make_terms(node_count, device_count, me_ref, rack_hbm, node_hbm, slots_hbm, coeff_hbm, stored_hbm,
               out_ref, racks, nodes, all_slots, coeffs, blocks, weight, sems):
    chunks, held_planes, columns = blocks.shape
    tiles = columns // LANES
    terms = REP_DEV * HELPERS
    planes = held_planes // terms
    index = [
        pltpu.make_async_copy(source, target, sems.at[n])
        for n, (source, target) in enumerate(
            ((rack_hbm.at[:, pl.ds(0, LANES)], racks), (node_hbm.at[:, pl.ds(0, LANES)], nodes),
             (slots_hbm, all_slots), (coeff_hbm, coeffs))
        )
    ]
    for copy in index:
        copy.start()
    loads = [
        pltpu.make_async_copy(stored_hbm.at[:, pl.ds(c * columns, columns)], blocks.at[c], sems.at[len(index) + c])
        for c in range(chunks)
    ]
    for copy in loads:
        copy.start()
    me = me_ref[0]
    repairs = all_slots.shape[1]
    width = weight.shape[0] * LANES
    entries = planes * planes
    repair = lax.broadcasted_iota(jnp.int32, (HELPERS, repairs), 1)
    own = lax.div(lax.broadcasted_iota(jnp.int32, (HELPERS, HELPERS * entries), 1), entries) == (
        lax.broadcasted_iota(jnp.int32, (HELPERS, HELPERS * entries), 0)
    )
    fold = (
        lax.rem(lax.broadcasted_iota(jnp.int32, (HELPERS * entries, entries), 0), entries)
        == lax.broadcasted_iota(jnp.int32, (HELPERS * entries, entries), 1)
    ).astype(jnp.bfloat16)
    entry = lax.broadcasted_iota(jnp.int32, (entries, width), 0)
    lane = lax.broadcasted_iota(jnp.int32, (entries, width), 1)
    slot_of_lane = lax.div(lax.broadcasted_iota(jnp.int32, (HELPERS, width), 1), planes)
    spreads = [
        (entry == p * planes + lax.rem(lane, planes)).astype(jnp.float32).astype(jnp.bfloat16) for p in range(planes)
    ]
    for copy in index:
        copy.wait()
    table = coeffs[...].reshape(HELPERS * entries, repairs)
    every_of, slots = [], []
    for s in range(REP_DEV):
        offset = lax.rem(racks[:, s : s + 1] * node_count + nodes[:, s : s + 1], device_count)
        row = lax.rem(me + device_count - offset, device_count) * REP_DEV + s
        chosen = row == repair
        slots.append(jnp.sum(jnp.where(chosen, all_slots[...], 0), axis=1, keepdims=True))
        every = lax.dot_general(
            chosen.astype(jnp.float32).astype(jnp.bfloat16), table, (((1,), (1,)), ((), ())),
            preferred_element_type=jnp.float32,
        )
        every_of.append(jnp.where(own, every, 0.0).astype(jnp.bfloat16))
    both = jnp.dot(jnp.concatenate(every_of, 0), fold, preferred_element_type=jnp.float32).astype(jnp.bfloat16)
    for p in range(planes):
        pair = jnp.dot(both, spreads[p], preferred_element_type=jnp.float32)
        for s in range(REP_DEV):
            wide = pair[s * HELPERS : (s + 1) * HELPERS]
            wide = jnp.where(slots[s] == slot_of_lane, wide, 0.0)
            first = (s * planes + p) * HELPERS
            for w in range(weight.shape[0]):
                weight[w, first : first + HELPERS, :] = wide[:, w * LANES : (w + 1) * LANES]
    matrix = jnp.concatenate([weight[w] for w in range(weight.shape[0])], 1)[:, :held_planes].astype(jnp.bfloat16)
    for c in range(chunks):
        loads[c].wait()
        result = jnp.dot(matrix, blocks[c], preferred_element_type=jnp.float32)
        for j in range(tiles):
            for s in range(REP_DEV):
                out_ref[s, c * tiles + j] = result[s * planes * HELPERS : (s + 1) * planes * HELPERS, j * LANES : (j + 1) * LANES]


def add_terms(node_count, device_count, me_ref, rack_any, node_any, held_any, out_ref, racks, nodes, held, sems):
    per = held_any.shape[0] // device_count
    parts = per // HELPERS
    index = [
        pltpu.make_async_copy(source.at[:, pl.ds(0, LANES)], target, sems.at[n])
        for n, (source, target) in enumerate(((rack_any, racks), (node_any, nodes)))
    ]
    main = pltpu.make_async_copy(held_any, held.at[pl.ds(0, device_count * per)], sems.at[2])
    wrap = pltpu.make_async_copy(
        held_any.at[pl.ds(0, TILE * per)], held.at[pl.ds(device_count * per, TILE * per)], sems.at[3]
    )
    for copy in index:
        copy.start()
    main.start()
    wrap.start()
    for copy in index:
        copy.wait()
    turn = TURN % device_count
    s = lax.div(lax.rem(me_ref[0] * turn, device_count), device_count // REP_DEV)
    offsets = [lax.rem((racks[h, s] * node_count + nodes[h, s]) * turn, device_count) for h in range(HELPERS)]
    main.wait()
    wrap.wait()

    @pl.loop(0, device_count // TILE, unroll=4)
    def _(j):
        starts = [lax.rem(j * TILE + offset, device_count) * per for offset in offsets]
        for i in range(parts):
            total = None
            for h in range(HELPERS):
                part = held[pl.ds(starts[h] + (i * HELPERS + h), TILE, stride=per), :]
                total = part if total is None else total + part
            out_ref[pl.ds(j * TILE * parts + i, TILE, stride=parts), :] = total


def deliver(in_any, out_any, sems):
    share = in_any.shape[2] // PIECES
    copies = [
        pltpu.make_async_copy(
            in_any.at[s, :, pl.ds(n * share, share)], out_any.at[s, :, pl.ds(n * share, share)], sems.at[s * PIECES + n]
        )
        for s in range(REP_DEV)
        for n in range(PIECES)
    ]
    for copy in copies:
        copy.start()
    for copy in copies:
        copy.wait()


def ring(count):
    order = [0] * count
    for device in range(count):
        order[device * TURN % count] = device
    return [order]


def on_device(stored, coefficients, helper_rack, helper_node, helper_block):
    node_count = lax.axis_size("node")
    device_count = lax.axis_size(AXES)
    held, planes, length = stored.shape
    terms = REP_DEV * HELPERS
    me = (lax.axis_index("rack") * node_count + lax.axis_index("node")).reshape(1)
    tiles = length // LANES
    chunks = 1
    racks, nodes, slots = helper_rack.T, helper_node.T, helper_block.T
    table = coefficients.transpose(1, 2, 3, 0)
    blocks = stored.reshape(held * planes, length)
    sent = pl.pallas_call(
        lambda *refs: make_terms(node_count, device_count, *refs),
        out_shape=jax.ShapeDtypeStruct((REP_DEV, tiles, planes * HELPERS, LANES), jnp.float32),
        in_specs=[pl.BlockSpec(memory_space=pltpu.SMEM)] + [pl.BlockSpec(memory_space=pl.ANY)] * 5,
        out_specs=pl.BlockSpec(memory_space=pltpu.VMEM),
        scratch_shapes=[
            pltpu.VMEM((HELPERS, LANES), jnp.int32),
            pltpu.VMEM((HELPERS, LANES), jnp.int32),
            pltpu.VMEM(slots.shape, jnp.int32),
            pltpu.VMEM(table.shape, table.dtype),
            pltpu.VMEM((chunks, held * planes, length // chunks), stored.dtype),
            pltpu.VMEM((pl.cdiv(held * planes, LANES), planes * terms, LANES), jnp.float32),
            pltpu.SemaphoreType.DMA((4 + chunks,)),
        ],
        compiler_params=pltpu.CompilerParams(vmem_limit_bytes=12 << 20),
        name="make_terms",
    )(me, *(pltpu.with_memory_space_constraint(x, pltpu.HBM) for x in (racks, nodes, slots, table, blocks)))
    per = REP_DEV * tiles * planes * HELPERS // device_count
    arrived = lax.all_to_all(sent.reshape(device_count, per, LANES), AXES, 0, 0, tiled=True, axis_index_groups=ring(device_count))
    parts = per // HELPERS
    back = pl.pallas_call(
        lambda *refs: add_terms(node_count, device_count, *refs),
        out_shape=jax.ShapeDtypeStruct((device_count * parts, LANES), jnp.float32),
        in_specs=[pl.BlockSpec(memory_space=pltpu.SMEM)] + [pl.BlockSpec(memory_space=pl.ANY)] * 3,
        out_specs=pl.BlockSpec(memory_space=pltpu.VMEM),
        scratch_shapes=[
            pltpu.SMEM((HELPERS, LANES), jnp.int32),
            pltpu.SMEM((HELPERS, LANES), jnp.int32),
            pltpu.VMEM(((device_count + TILE) * per, LANES), jnp.float32),
            pltpu.SemaphoreType.DMA((4,)),
        ],
        compiler_params=pltpu.CompilerParams(vmem_limit_bytes=12 << 20),
        name="add_terms",
    )(me, racks, nodes, arrived.reshape(device_count * per, LANES))
    home = lax.all_to_all(back.reshape(device_count, parts, LANES), AXES, 0, 0, tiled=True, axis_index_groups=ring(device_count))
    home = home.reshape(REP_DEV, tiles, planes, LANES).transpose(0, 2, 1, 3)
    return pl.pallas_call(
        deliver,
        out_shape=jax.ShapeDtypeStruct((REP_DEV, planes, length), jnp.float32),
        in_specs=[pl.BlockSpec(memory_space=pl.ANY)],
        out_specs=pl.BlockSpec(memory_space=pl.ANY),
        scratch_shapes=[pltpu.SemaphoreType.DMA((REP_DEV * PIECES,))],
        compiler_params=pltpu.CompilerParams(vmem_limit_bytes=4 << 20),
        name="deliver",
    )(home.reshape(REP_DEV, planes, length))


def solution(mesh):
    placed = (P(AXES, None, None), P(), P(), P(), P())
    return jax.shard_map(
        on_device,
        mesh=mesh,
        in_specs=placed,
        out_specs=P(AXES, None, None),
        check_vma=False,
    )
```

```python
import jax
import jax.numpy as jnp
from jax import lax
from jax.experimental import pallas as pl
from jax.experimental.pallas import tpu as pltpu
from jax.sharding import PartitionSpec as P

HELPERS = 10
REP_DEV = 2
AXES = ("rack", "node")
LANES = 128
TILE = 8
TURN = 101


def offset_of(rack_ref, node_ref, node_count, device_count, s, h):
    return lax.rem(rack_ref[h, s] * node_count + node_ref[h, s], device_count)


def make_terms(node_count, device_count, me_ref, rack_hbm, node_hbm, slots_hbm, coeff_hbm, stored_hbm,
               out_ref, racks, nodes, all_slots, coeffs, blocks, weight, sems):
    chunks, held_planes, columns = blocks.shape
    tiles = columns // LANES
    terms = REP_DEV * HELPERS
    planes = held_planes // terms
    index = [
        pltpu.make_async_copy(source, target, sems.at[n])
        for n, (source, target) in enumerate(
            ((coeff_hbm, coeffs), (rack_hbm.at[:, pl.ds(0, LANES)], racks),
             (node_hbm.at[:, pl.ds(0, LANES)], nodes), (slots_hbm, all_slots))
        )
    ]
    for copy in index:
        copy.start()
    loads = [
        pltpu.make_async_copy(stored_hbm.at[:, pl.ds(c * columns, columns)], blocks.at[c], sems.at[len(index) + c])
        for c in range(chunks)
    ]
    for copy in loads:
        copy.start()
    me = me_ref[0]
    repairs = all_slots.shape[1]
    width = weight.shape[0] * LANES
    entries = planes * planes
    repair = lax.broadcasted_iota(jnp.int32, (HELPERS, repairs), 1)
    own = lax.div(lax.broadcasted_iota(jnp.int32, (HELPERS, HELPERS * entries), 1), entries) == (
        lax.broadcasted_iota(jnp.int32, (HELPERS, HELPERS * entries), 0)
    )
    fold = (
        lax.rem(lax.broadcasted_iota(jnp.int32, (HELPERS * entries, entries), 0), entries)
        == lax.broadcasted_iota(jnp.int32, (HELPERS * entries, entries), 1)
    ).astype(jnp.bfloat16)
    entry = lax.broadcasted_iota(jnp.int32, (entries, width), 0)
    lane = lax.broadcasted_iota(jnp.int32, (entries, width), 1)
    slot_of_lane = lax.div(lax.broadcasted_iota(jnp.int32, (HELPERS, width), 1), planes)
    spreads = [
        (entry == p * planes + lax.rem(lane, planes)).astype(jnp.float32).astype(jnp.bfloat16) for p in range(planes)
    ]
    for copy in index:
        copy.wait()
    table = coeffs[...].reshape(HELPERS * entries, repairs)
    every_of, slots = [], []
    for s in range(REP_DEV):
        offset = lax.rem(racks[:, s : s + 1] * node_count + nodes[:, s : s + 1], device_count)
        row = lax.rem(me + device_count - offset, device_count) * REP_DEV + s
        chosen = row == repair
        slots.append(jnp.sum(jnp.where(chosen, all_slots[...], 0), axis=1, keepdims=True))
        every = lax.dot_general(
            chosen.astype(jnp.float32).astype(jnp.bfloat16), table, (((1,), (1,)), ((), ())),
            preferred_element_type=jnp.float32,
        )
        every_of.append(jnp.where(own, every, 0.0).astype(jnp.bfloat16))
    both = jnp.dot(jnp.concatenate(every_of, 0), fold, preferred_element_type=jnp.float32).astype(jnp.bfloat16)
    for p in range(planes):
        pair = jnp.dot(both, spreads[p], preferred_element_type=jnp.float32)
        for s in range(REP_DEV):
            wide = pair[s * HELPERS : (s + 1) * HELPERS]
            wide = jnp.where(slots[s] == slot_of_lane, wide, 0.0)
            first = (s * planes + p) * HELPERS
            for w in range(weight.shape[0]):
                weight[w, first : first + HELPERS, :] = wide[:, w * LANES : (w + 1) * LANES]
    matrix = jnp.concatenate([weight[w] for w in range(weight.shape[0])], 1)[:, :held_planes].astype(jnp.bfloat16)
    for c in range(chunks):
        loads[c].wait()
        result = jnp.dot(matrix, blocks[c], preferred_element_type=jnp.float32)
        for j in range(tiles):
            for s in range(REP_DEV):
                out_ref[s, c * tiles + j] = result[s * planes * HELPERS : (s + 1) * planes * HELPERS, j * LANES : (j + 1) * LANES]


def add_terms(node_count, device_count, me_ref, rack_any, node_any, held_any, out_ref, racks, nodes, held, sems):
    per = held_any.shape[0] // device_count
    parts = per // HELPERS
    index = [
        pltpu.make_async_copy(source.at[:, pl.ds(0, LANES)], target, sems.at[n])
        for n, (source, target) in enumerate(((rack_any, racks), (node_any, nodes)))
    ]
    main = pltpu.make_async_copy(held_any, held.at[pl.ds(0, device_count * per)], sems.at[2])
    wrap = pltpu.make_async_copy(
        held_any.at[pl.ds(0, TILE * per)], held.at[pl.ds(device_count * per, TILE * per)], sems.at[3]
    )
    for copy in index:
        copy.start()
    main.start()
    wrap.start()
    for copy in index:
        copy.wait()
    turn = TURN % device_count
    s = lax.div(lax.rem(me_ref[0] * turn, device_count), device_count // REP_DEV)
    offsets = [lax.rem((racks[h, s] * node_count + nodes[h, s]) * turn, device_count) for h in range(HELPERS)]
    main.wait()
    wrap.wait()

    @pl.loop(0, device_count // TILE, unroll=4)
    def _(j):
        starts = [lax.rem(j * TILE + offset, device_count) * per for offset in offsets]
        for i in range(parts):
            total = None
            for h in range(HELPERS):
                part = held[pl.ds(starts[h] + (i * HELPERS + h), TILE, stride=per), :]
                total = part if total is None else total + part
            out_ref[pl.ds(j * TILE * parts + i, TILE, stride=parts), :] = total


def ring(count):
    order = [0] * count
    for device in range(count):
        order[device * TURN % count] = device
    return [order]


def on_device(stored, coefficients, helper_rack, helper_node, helper_block):
    node_count = lax.axis_size("node")
    device_count = lax.axis_size(AXES)
    held, planes, length = stored.shape
    terms = REP_DEV * HELPERS
    me = (lax.axis_index("rack") * node_count + lax.axis_index("node")).reshape(1)
    tiles = length // LANES
    chunks = 1
    racks, nodes, slots = helper_rack.T, helper_node.T, helper_block.T
    table = coefficients.transpose(1, 2, 3, 0)
    blocks = stored.reshape(held * planes, length)
    sent = pl.pallas_call(
        lambda *refs: make_terms(node_count, device_count, *refs),
        out_shape=jax.ShapeDtypeStruct((REP_DEV, tiles, planes * HELPERS, LANES), jnp.float32),
        in_specs=[pl.BlockSpec(memory_space=pltpu.SMEM)] + [pl.BlockSpec(memory_space=pl.ANY)] * 5,
        out_specs=pl.BlockSpec(memory_space=pltpu.VMEM),
        scratch_shapes=[
            pltpu.VMEM((HELPERS, LANES), jnp.int32),
            pltpu.VMEM((HELPERS, LANES), jnp.int32),
            pltpu.VMEM(slots.shape, jnp.int32),
            pltpu.VMEM(table.shape, table.dtype),
            pltpu.VMEM((chunks, held * planes, length // chunks), stored.dtype),
            pltpu.VMEM((pl.cdiv(held * planes, LANES), planes * terms, LANES), jnp.float32),
            pltpu.SemaphoreType.DMA((4 + chunks,)),
        ],
        compiler_params=pltpu.CompilerParams(vmem_limit_bytes=12 << 20),
        name="make_terms",
    )(me, *(pltpu.with_memory_space_constraint(x, pltpu.HBM) for x in (racks, nodes, slots, table, blocks)))
    per = REP_DEV * tiles * planes * HELPERS // device_count
    arrived = lax.all_to_all(sent.reshape(device_count, per, LANES), AXES, 0, 0, tiled=True, axis_index_groups=ring(device_count))
    parts = per // HELPERS
    back = pl.pallas_call(
        lambda *refs: add_terms(node_count, device_count, *refs),
        out_shape=jax.ShapeDtypeStruct((device_count * parts, LANES), jnp.float32),
        in_specs=[pl.BlockSpec(memory_space=pltpu.SMEM)] + [pl.BlockSpec(memory_space=pl.ANY)] * 3,
        out_specs=pl.BlockSpec(memory_space=pltpu.VMEM),
        scratch_shapes=[
            pltpu.SMEM((HELPERS, LANES), jnp.int32),
            pltpu.SMEM((HELPERS, LANES), jnp.int32),
            pltpu.VMEM(((device_count + TILE) * per, LANES), jnp.float32),
            pltpu.SemaphoreType.DMA((4,)),
        ],
        compiler_params=pltpu.CompilerParams(vmem_limit_bytes=12 << 20),
        name="add_terms",
    )(me, racks, nodes, arrived.reshape(device_count * per, LANES))
    home = lax.all_to_all(back.reshape(device_count, parts, LANES), AXES, 0, 0, tiled=True, axis_index_groups=ring(device_count))
    home = home.reshape(REP_DEV, tiles, planes, LANES).transpose(0, 2, 1, 3)
    return home.reshape(REP_DEV, planes, length)


def solution(mesh):
    placed = (P(AXES, None, None), P(), P(), P(), P())
    return jax.shard_map(
        on_device,
        mesh=mesh,
        in_specs=placed,
        out_specs=P(AXES, None, None),
        check_vma=False,
    )
```
